256 devices in a mesh: dp: 4 (over x), mp: 64 (over z, y, core).
Axes of the slice: x: 4, y: 4, z: 8, core: 2. Of those that a mesh axis runs over, the one named last changes fastest.
Arguments:
- residual: bfloat16 [1024, 4096], P(('dp', 'mp')), may hold values from -6 to 6
- ffn_gain: float32 [4096], replicated, may hold values from 0.5 to 1.5
- gate_weight: bfloat16 [4096, 8192], P(None, 'mp'), may hold values from -0.09375 to 0.09375
- up_weight: bfloat16 [4096, 8192], P(None, 'mp'), may hold values from -0.09375 to 0.09375
- down_weight: bfloat16 [8192, 4096], P('mp'), may hold values from -0.0625 to 0.0625
- final_gain: float32 [4096], replicated, may hold values from 0.5 to 1.5
- head_weight: bfloat16 [4096, 65536], P(None, 'mp')
- passage_ids: int32 [4, 256], P('dp'), may hold values from 0 to 3, never falling along the last dimension, each value on 1 to 128 neighbouring positions
- valid_counts: int32 [4, 4], P('dp'), may hold values from 1 to 128
Outputs:
- term_weights: float32 [16, 65536], P('dp', 'mp')
- entropy: float32 [], replicated
- grad_hidden: float32 [1024, 4096], P(('dp', 'mp'))
The draws below stay inside these ranges and needn't reach their ends.
Inputs may be any that keep to these rules, and one draw needn't show every extreme that they name: `passage_ids`: within each group the ids never fall and every passage of 0 to 3 has 1 to 128 rows.
All inputs are finite; a program needn't handle non-finite values.
Results may differ from the reference program's by a relative error of at most 0.0069.
The reference program's roundings to bfloat16 on the way (of `normed_in`, `activated`, `normed` and `slope_logit`) count: a program that leaves them out, or rounds other values in their place, can miss the bound.
Values may be sent and summed in bfloat16 or wider, within the bound.
No kernel may reach another device: no remote copies, remote signals or barrier semaphores. Data moves between devices by JAX's collectives and lax.ppermute only.
A program may use at most 64 MiB of HBM per device.

```python
import math
import jax
import jax.numpy as jnp
import numpy as np
from jax import lax

D = 4096
FF = 8192
V = 65536
ROWS = 256
PASS = 4
MOST = 128
TOKENS = 1024
N_DP = 4


def draw_head_weight(key, part):
    column = jnp.arange(V, dtype=jnp.float32) / float(V - 1)
    entries = jax.random.truncated_normal(key, -6.0, 6.0, (D, V), jnp.float32)
    lowest = 0.5
    highest = 4.0
    column_scale = jnp.exp(math.log(lowest) + column * math.log(highest / lowest))
    values = entries * column_scale[None, :] * float(D) ** (-0.5)
    return values.astype(jnp.bfloat16)


def place_ends(array, own_key, smallest, high):
    dims = array.shape
    spot = [jax.random.randint(jax.random.fold_in(own_key, axis), (), 0, dims[axis]) for axis in range(len(dims))]
    array = array.at[tuple(spot)].set(smallest)
    longest = dims.index(max(dims))
    spot[longest] = (spot[longest] + 1) % dims[longest]
    return array.at[tuple(spot)].set(high)


def block_scale(key, extent, shards, least, high):
    loudness = 1.0
    for axis_at, blocks in shards:
        heights = jax.random.uniform(jax.random.fold_in(jax.random.fold_in(key, 6), axis_at), (blocks,), jnp.float32, least / len(shards), high / len(shards))
        loudness = loudness * jnp.repeat(jnp.exp(heights), extent[axis_at] // blocks).reshape((-1,) + (1,) * (len(extent) - 1 - axis_at))
    return loudness


def split_up(amount, total, limit, lean):
    weights = [(1 << 20) // math.isqrt(standing ** lean) + 1 for standing in range(2, amount + 1)]
    spare, given = total - limit - (amount - 1), [1] * (amount - 1)
    while spare > 0:
        free = [i for i in range(amount - 1) if given[i] < limit]
        mass, left = sum([weights[i] for i in free]), spare
        for i in free:
            more = min(limit - given[i], max(1, left * weights[i] // mass), spare)
            given[i] = given[i] + more
            spare = spare - more
    return np.array([limit] + given)


def uneven(key, count, total, most, skew):
    if count == 2:
        one = jax.random.randint(key, (), max(1, total - most), min(most, total - 1) + 1)
        return jnp.stack([one, total - one])
    lengths = jnp.asarray(split_up(count, total, most, skew), jnp.int32)
    twos = (count - 1) // 2
    giver, taker = lengths[1:1 + 2 * twos:2], lengths[2:2 + 2 * twos:2]
    room = jnp.minimum(giver - 1, most - taker)
    passed = jax.random.randint(jax.random.fold_in(key, 1), (twos,), 0, 1 << 20) % (room + 1)
    lengths = lengths.at[1:1 + 2 * twos:2].set(giver - passed).at[2:2 + 2 * twos:2].set(taker + passed)
    return lengths[jax.random.permutation(jax.random.fold_in(key, 2), count)]


def noise(key, dims, deviation, bound, split=(), held_as=jnp.bfloat16):
    array = deviation * jax.random.normal(key, dims, jnp.float32)
    if split:
        array = array * block_scale(key, dims, split, -0.22, 0.18)
    return jnp.clip(array, -bound, bound).astype(held_as)


def setup_inputs(seed: int = 0) -> dict:
    seeds = jax.random.split(jax.random.key(seed), 10)
    return {
        "residual": noise(seeds[0], (TOKENS, D), 1.0, 6.0, ((0, 256),)),
        "ffn_gain": jnp.clip(1.0 + 0.1 * jax.random.normal(seeds[1], (D,), jnp.float32), 0.5, 1.5),
        "gate_weight": noise(seeds[2], (D, FF), D ** -0.5, 0.09375, ((1, 64),)),
        "up_weight": noise(seeds[3], (D, FF), D ** -0.5, 0.09375, ((1, 64),)),
        "down_weight": noise(seeds[4], (FF, D), FF ** -0.5, 0.0625, ((0, 64),)),
        "final_gain": jnp.clip(1.0 + 0.1 * jax.random.normal(seeds[5], (D,), jnp.float32), 0.5, 1.5),
        "head_weight": draw_head_weight(jax.random.fold_in(seeds[9], 71), 0),
        "passage_ids": jax.vmap(lambda own: jnp.searchsorted(jnp.cumsum(uneven(own, PASS, ROWS, MOST, 1)), jnp.arange(ROWS), side="right"))(jax.random.split(seeds[7], N_DP)).reshape((N_DP, ROWS)).astype(jnp.int32),
        "valid_counts": place_ends(jax.random.randint(seeds[8], (N_DP, PASS), 1, MOST + 1), jax.random.fold_in(seeds[8], 1), 1, MOST).astype(jnp.int32),
    }


def rms_scale(values):
    return lax.rsqrt(lax.optimization_barrier(jnp.mean(values * values, axis=-1, keepdims=True)) + 1e-05)

def pool_masks(ids, counts):
    slots = jnp.arange(counts.shape[0], dtype=jnp.int32)
    member = ids[:, None] == slots[None, :]
    starts = lax.optimization_barrier(jnp.sum((ids[:, None] < slots[None, :]).astype(jnp.int32), axis=0))
    start_row = lax.optimization_barrier(jnp.sum(jnp.where(member, starts[None, :], 0), axis=1)).astype(jnp.int32)
    count_row = lax.optimization_barrier(jnp.sum(jnp.where(member, counts[None, :], 0), axis=1)).astype(jnp.int32)
    position = jnp.arange(ids.shape[0], dtype=jnp.int32) - start_row
    valid = (position < count_row).astype(jnp.float32)
    return (member.astype(jnp.float32), valid)

def reference(residual, ffn_gain, gate_weight, up_weight, down_weight, final_gain, head_weight, passage_ids, valid_counts):
    highest = lax.Precision.HIGHEST
    kept = []
    pooled_list = []
    for group_index in range(N_DP):
        row_block = residual[group_index * ROWS:(group_index + 1) * ROWS].astype(jnp.float32)
        normed_in = (row_block * rms_scale(row_block) * ffn_gain).astype(jnp.bfloat16)
        gate_vals = jnp.dot(normed_in, gate_weight, preferred_element_type=jnp.float32)
        up_vals = jnp.dot(normed_in, up_weight, preferred_element_type=jnp.float32)
        activated = (jax.nn.silu(gate_vals) * up_vals).astype(jnp.bfloat16)
        hidden = row_block + jnp.dot(activated, down_weight, preferred_element_type=jnp.float32)
        scale = rms_scale(hidden)
        normed = (hidden * scale * final_gain).astype(jnp.bfloat16)
        logits = jnp.dot(normed, head_weight, preferred_element_type=jnp.float32)
        member, valid = pool_masks(passage_ids[group_index], valid_counts[group_index])
        weights = jnp.log1p(jnp.maximum(logits, 0.0))
        powered = valid[:, None] * weights ** 4
        pooled_sum = jnp.dot(member.T, powered, precision=highest)
        kept.append((hidden, scale, logits, weights, member, valid, pooled_sum))
        pooled_list.append(pooled_sum)
    pooled_all = jnp.concatenate(pooled_list, axis=0)
    term_weights = (1.0 + pooled_all) ** 0.25 - 1.0
    smooth = 1.0 + lax.optimization_barrier(jnp.sum(term_weights, axis=0))
    total = jnp.sum(smooth)
    spread = jnp.sum(smooth * jnp.log(smooth))
    entropy = jnp.log(total) - spread / total
    slope_mass = jnp.log(total) - jnp.log(smooth)
    grads = []
    for hidden, scale, logits, weights, member, valid, pooled_sum in kept:
        factor = (1.0 + pooled_sum) ** (-0.75)
        row_factor = jnp.dot(member, factor, precision=highest)
        slope_logit = (valid[:, None] * weights ** 3 * row_factor * slope_mass[None, :] / (1.0 + jnp.maximum(logits, 0.0))).astype(jnp.bfloat16)
        slope_normed = jnp.dot(slope_logit, head_weight.T, preferred_element_type=jnp.float32)
        scaled_slope = slope_normed * final_gain
        grads.append(scale * scaled_slope - hidden * scale ** 3 * lax.optimization_barrier(jnp.mean(scaled_slope * hidden, axis=-1, keepdims=True)))
    grad_hidden = jnp.concatenate(grads, axis=0)
    return (term_weights, entropy, grad_hidden)
```

```python
import jax
import jax.numpy as jnp
from jax import lax
from jax.sharding import Mesh, PartitionSpec as P


CHUNKS = 2
PLANE = ("z", "y")
ALL = ("dp", "z", "y", "c")
MP = ("z", "y", "c")
BF = jnp.bfloat16
F32 = jnp.float32


def rms_scale(values):
    return lax.rsqrt(jnp.mean(values * values, axis=-1, keepdims=True) + 1e-05)


def pool_masks(ids, counts):
    slots = jnp.arange(counts.shape[0], dtype=jnp.int32)
    member = ids[:, None] == slots[None, :]
    starts = jnp.sum((ids[:, None] < slots[None, :]).astype(jnp.int32), axis=0)
    start_row = jnp.sum(jnp.where(member, starts[None, :], 0), axis=1)
    count_row = jnp.sum(jnp.where(member, counts[None, :], 0), axis=1)
    position = jnp.arange(ids.shape[0], dtype=jnp.int32) - start_row
    valid = (position < count_row).astype(F32)
    return (member.astype(F32), valid)


def swap(x):
    return lax.ppermute(x, "c", [(0, 1), (1, 0)])


def mm(a, b):
    return jnp.dot(a, b, preferred_element_type=F32)


def mm_t(a, b):
    return lax.dot_general(a, b, (((1,), (1,)), ((), ())), preferred_element_type=F32)


def halves(x, core, axis):
    size = x.shape[axis] // 2
    own = lax.dynamic_slice_in_dim(x, core * size, size, axis)
    other = lax.dynamic_slice_in_dim(x, (1 - core) * size, size, axis)
    return own, other


def pieces(x, axis):
    return jnp.split(x, CHUNKS, axis=axis)


def chip_rows(x, core):
    own, other = halves(x, core, 1)
    got = swap(other)
    return jnp.where(core == 0, jnp.concatenate([own, got], 0), jnp.concatenate([got, own], 0))


def core_rows(x, core):
    own, other = halves(x, core, 0)
    got = swap(other)
    return jnp.where(core == 0, jnp.concatenate([own, got], 1), jnp.concatenate([got, own], 1))


def gather(block, n):
    spread = jnp.broadcast_to(block[None], (n, *block.shape))
    rows = lax.all_to_all(spread, PLANE, 0, 0).reshape(-1, block.shape[-1])
    mine = pieces(rows, 1)
    theirs = [swap(m) for m in mine]
    return mine, theirs


def scatter(own_parts, other_parts, n):
    got = [swap(p) for p in other_parts]
    both = jnp.concatenate(
        [(own + recv.astype(F32)).astype(BF) for own, recv in zip(own_parts, got)], axis=1
    )
    moved = lax.all_to_all(both.reshape(n, -1, both.shape[-1]), PLANE, 0, 0)
    return jnp.sum(moved.astype(F32), axis=0)


def body(
    residual,
    ffn_gain,
    gate_weight,
    up_weight,
    down_weight,
    final_gain,
    head_weight,
    passage_ids,
    valid_counts,
):
    highest = lax.Precision.HIGHEST
    core = lax.axis_index("c")
    n = lax.axis_size(PLANE)
    n_dp = lax.axis_size("dp")
    n_mp = lax.axis_size(MP)
    own_rows = residual.astype(F32)
    normed_in = (own_rows * rms_scale(own_rows) * ffn_gain).astype(BF)
    mine, theirs = gather(chip_rows(normed_in, core), n)
    residual8 = chip_rows(residual, core).astype(F32)
    gain8 = halves(final_gain[None, :], core, 1)[0]

    gate_up = jnp.concatenate([gate_weight, up_weight], axis=1)
    gu_own, gu_other = halves(gate_up, core, 0)
    gu = sum(
        mm(a, b)
        for a, b in zip(mine + theirs, pieces(gu_own, 0) + pieces(gu_other, 0))
    )
    hid = gate_weight.shape[1]
    activated = (jax.nn.silu(gu[:, :hid]) * gu[:, hid:]).astype(BF)
    down_own, down_other = halves(down_weight, core, 1)
    others = [mm(activated, w).astype(BF) for w in pieces(down_other, 1)]
    owns = [mm(activated, w) for w in pieces(down_own, 1)]
    hidden8 = residual8 + scatter(owns, others, n)
    square = jnp.sum(hidden8 * hidden8, axis=1, keepdims=True)
    width = residual.shape[1]
    scale8 = lax.rsqrt((square + swap(square)) / width + 1e-05)
    normed8 = (hidden8 * scale8 * gain8).astype(BF)
    mine, theirs = gather(normed8, n)
    hidden = core_rows(hidden8, core)

    head_own, head_other = halves(head_weight, core, 0)
    logits = sum(
        mm(a, b)
        for a, b in zip(mine + theirs, pieces(head_own, 0) + pieces(head_other, 0))
    )
    member, valid = pool_masks(passage_ids[0], valid_counts[0])
    weights = jnp.log1p(jnp.maximum(logits, 0.0))
    powered = valid[:, None] * weights**4
    pooled_sum = lax.dot_general(member, powered, (((0,), (0,)), ((), ())), precision=highest)
    term_weights = (1.0 + pooled_sum) ** 0.25 - 1.0
    local_mass = jnp.sum(term_weights, axis=0).reshape(1, -1, 128)
    masses = lax.all_to_all(jnp.broadcast_to(local_mass, (n_dp, *local_mass.shape[1:])), "dp", 0, 0)
    smooth = 1.0 + jnp.sum(masses, axis=0).reshape(-1)
    log_smooth = jnp.log(smooth)
    lane = jnp.arange(128)
    sums = jnp.where(lane == 0, jnp.sum(smooth), jnp.where(lane == 1, jnp.sum(smooth * log_smooth), 0.0))
    sums = lax.all_to_all(jnp.broadcast_to(sums, (n_mp, 1, 128)), MP, 0, 0)
    sums = jnp.sum(sums, axis=(0, 1))
    total, spread = sums[0], sums[1]
    entropy = jnp.log(total) - spread / total
    slope_mass = jnp.log(total) - log_smooth
    factor = (1.0 + pooled_sum) ** (-0.75)
    row_factor = jnp.dot(member, factor, precision=highest)
    slope_logit = (
        valid[:, None]
        * weights**3
        * row_factor
        * slope_mass[None, :]
        / (1.0 + jnp.maximum(logits, 0.0))
    ).astype(BF)
    others = [mm_t(slope_logit, w).astype(BF) for w in pieces(head_other, 0)]
    owns = [mm_t(slope_logit, w) for w in pieces(head_own, 0)]
    slope_normed = core_rows(scatter(owns, others, n), core)
    scaled_slope = slope_normed * final_gain
    scale = rms_scale(hidden)
    grad_hidden = scale * scaled_slope - hidden * scale**3 * jnp.mean(
        scaled_slope * hidden, axis=-1, keepdims=True
    )
    return (term_weights, entropy, grad_hidden)


def solution(mesh):
    axes = Mesh(mesh.devices.reshape(mesh.shape["dp"], 8, 4, 2), ALL)
    placed = (
        P(ALL, None),
        P(),
        P(None, MP),
        P(None, MP),
        P(MP, None),
        P(),
        P(None, MP),
        P("dp", None),
        P("dp", None),
    )
    return jax.shard_map(
        body,
        mesh=axes,
        in_specs=placed,
        out_specs=(P("dp", MP), P(), P(ALL, None)),
        check_vma=False,
    )
```

```python
import jax
import jax.numpy as jnp
from jax import lax
from jax.sharding import Mesh, PartitionSpec as P


PLANE = ("z", "y")
ALL = ("dp", "z", "y", "c")
MP = ("z", "y", "c")
BF = jnp.bfloat16
F32 = jnp.float32


def rms_scale(values):
    return lax.rsqrt(jnp.mean(values * values, axis=-1, keepdims=True) + 1e-05)


def pool_masks(ids, counts):
    slots = jnp.arange(counts.shape[0], dtype=jnp.int32)
    member = ids[:, None] == slots[None, :]
    starts = jnp.sum((ids[:, None] < slots[None, :]).astype(jnp.int32), axis=0)
    start_row = jnp.sum(jnp.where(member, starts[None, :], 0), axis=1)
    count_row = jnp.sum(jnp.where(member, counts[None, :], 0), axis=1)
    position = jnp.arange(ids.shape[0], dtype=jnp.int32) - start_row
    valid = (position < count_row).astype(F32)
    return (member.astype(F32), valid)


def swap(x):
    return lax.ppermute(x, "c", [(0, 1), (1, 0)])


def mm(a, b):
    return jnp.dot(a, b, preferred_element_type=F32)


def mm_t(a, b):
    return lax.dot_general(a, b, (((1,), (1,)), ((), ())), preferred_element_type=F32)


def halves(x, core, axis):
    size = x.shape[axis] // 2
    own = lax.dynamic_slice_in_dim(x, core * size, size, axis)
    other = lax.dynamic_slice_in_dim(x, (1 - core) * size, size, axis)
    return own, other


def chip_rows(x, core):
    own, other = halves(x, core, 1)
    got = swap(other)
    return jnp.where(core == 0, jnp.concatenate([own, got], 0), jnp.concatenate([got, own], 0))


def core_rows(x, core):
    own, other = halves(x, core, 0)
    got = swap(other)
    return jnp.where(core == 0, jnp.concatenate([own, got], 1), jnp.concatenate([got, own], 1))


def exchange(x, axes):
    return lax.all_to_all(x, axes, 0, 0)


def gather(block, n):
    spread = jnp.broadcast_to(block[None], (n, *block.shape))
    mine = exchange(spread, PLANE).reshape(-1, block.shape[-1])
    return mine, swap(mine)


def scatter(own, other, n):
    both = (own + swap(other).astype(F32)).astype(BF)
    moved = exchange(both.reshape(n, -1, both.shape[-1]), PLANE)
    return jnp.sum(moved.astype(F32), axis=0)


def body(
    residual,
    ffn_gain,
    gate_weight,
    up_weight,
    down_weight,
    final_gain,
    head_weight,
    passage_ids,
    valid_counts,
):
    highest = lax.Precision.HIGHEST
    core = lax.axis_index("c")
    n = lax.axis_size(PLANE)
    n_dp = lax.axis_size("dp")
    n_mp = lax.axis_size(MP)
    own_rows = residual.astype(F32)
    normed_in = (own_rows * rms_scale(own_rows) * ffn_gain).astype(BF)
    member, valid = pool_masks(passage_ids[0], valid_counts[0])
    gate_up = jnp.concatenate([gate_weight, up_weight], axis=1)
    mine, theirs = gather(chip_rows(normed_in, core), n)
    residual8 = chip_rows(residual, core).astype(F32)
    gain8 = halves(final_gain[None, :], core, 1)[0]

    gu_own, gu_other = halves(gate_up, core, 0)
    gu = mm(mine, gu_own) + mm(theirs, gu_other)
    hid = gate_weight.shape[1]
    activated = (jax.nn.silu(gu[:, :hid]) * gu[:, hid:]).astype(BF)
    down_own, down_other = halves(down_weight, core, 1)
    other = mm(activated, down_other).astype(BF)
    hidden8 = residual8 + scatter(mm(activated, down_own), other, n)
    square = jnp.sum(hidden8 * hidden8, axis=1, keepdims=True)
    width = residual.shape[1]
    scale8 = lax.rsqrt((square + swap(square)) / width + 1e-05)
    normed8 = (hidden8 * scale8 * gain8).astype(BF)
    mine, theirs = gather(normed8, n)
    hidden = core_rows(hidden8, core)
    scale = rms_scale(hidden)

    head_own, head_other = halves(head_weight, core, 0)
    logits = mm(mine, head_own) + mm(theirs, head_other)
    positive = jnp.maximum(logits, 0.0)
    weights = jnp.log1p(positive)
    powered = valid[:, None] * weights**4
    pooled_sum = lax.dot_general(member, powered, (((0,), (0,)), ((), ())), precision=highest)
    term_weights = (1.0 + pooled_sum) ** 0.25 - 1.0
    local_mass = jnp.sum(term_weights, axis=0).reshape(1, -1, 128)
    masses = exchange(jnp.broadcast_to(local_mass, (n_dp, *local_mass.shape[1:])), "dp")
    slope = lax.optimization_barrier(valid[:, None] * weights**3 / (1.0 + positive))
    smooth = 1.0 + jnp.sum(masses, axis=0).reshape(-1)
    log_smooth = jnp.log(smooth)
    lane = jnp.arange(128)
    sums = jnp.where(lane == 0, jnp.sum(smooth), jnp.where(lane == 1, jnp.sum(smooth * log_smooth), 0.0))
    sums = exchange(jnp.broadcast_to(sums, (n_mp, 1, 128)), MP)
    row_factor = jnp.dot(member, (1.0 + pooled_sum) ** (-0.75), precision=highest)
    slope = lax.optimization_barrier(slope * row_factor)
    sums = jnp.sum(sums, axis=(0, 1))
    total, spread = sums[0], sums[1]
    entropy = jnp.log(total) - spread / total
    slope_mass = jnp.log(total) - log_smooth
    slope_logit = lax.optimization_barrier((slope * slope_mass[None, :]).astype(BF))
    other = mm_t(slope_logit, head_other).astype(BF)
    slope_normed = core_rows(scatter(mm_t(slope_logit, head_own), other, n), core)
    scaled_slope = slope_normed * final_gain
    grad_hidden = scale * scaled_slope - hidden * scale**3 * jnp.mean(
        scaled_slope * hidden, axis=-1, keepdims=True
    )
    return (term_weights, entropy, grad_hidden)


def solution(mesh):
    axes = Mesh(mesh.devices.reshape(mesh.shape["dp"], 8, 4, 2), ALL)
    placed = (
        P(ALL, None),
        P(),
        P(None, MP),
        P(None, MP),
        P(MP, None),
        P(),
        P(None, MP),
        P("dp", None),
        P("dp", None),
    )
    return jax.shard_map(
        body,
        mesh=axes,
        in_specs=placed,
        out_specs=(P("dp", MP), P(), P(ALL, None)),
        check_vma=False,
    )
```

```python
import jax
import jax.numpy as jnp
from jax import lax
from jax.sharding import Mesh, PartitionSpec as P


PLANE = ("z", "y")
ALL = ("dp", "z", "y", "c")
MP = ("z", "y", "c")
BF = jnp.bfloat16
F32 = jnp.float32


def rms_scale(values):
    return lax.rsqrt(jnp.mean(values * values, axis=-1, keepdims=True) + 1e-05)


def pool_masks(ids, counts):
    slots = jnp.arange(counts.shape[0], dtype=jnp.int32)
    member = ids[:, None] == slots[None, :]
    starts = jnp.sum((ids[:, None] < slots[None, :]).astype(jnp.int32), axis=0)
    start_row = jnp.sum(jnp.where(member, starts[None, :], 0), axis=1)
    count_row = jnp.sum(jnp.where(member, counts[None, :], 0), axis=1)
    position = jnp.arange(ids.shape[0], dtype=jnp.int32) - start_row
    valid = (position < count_row).astype(F32)
    return (member.astype(F32), valid)


def swap(x):
    return lax.ppermute(x, "c", [(0, 1), (1, 0)])


def mm(a, b):
    return jnp.dot(a, b, preferred_element_type=F32)


def mm_t(a, b):
    return lax.dot_general(a, b, (((1,), (1,)), ((), ())), preferred_element_type=F32)


def halves(x, core, axis):
    size = x.shape[axis] // 2
    own = lax.dynamic_slice_in_dim(x, core * size, size, axis)
    other = lax.dynamic_slice_in_dim(x, (1 - core) * size, size, axis)
    return own, other


def chip_rows(x, core):
    own, other = halves(x, core, 1)
    got = swap(other)
    return jnp.where(core == 0, jnp.concatenate([own, got], 0), jnp.concatenate([got, own], 0))


def core_rows(x, core):
    own, other = halves(x, core, 0)
    got = swap(other)
    return jnp.where(core == 0, jnp.concatenate([own, got], 1), jnp.concatenate([got, own], 1))


def exchange(x, axes):
    return lax.all_to_all(x, axes, 0, 0)


def gather(block, n):
    spread = jnp.broadcast_to(block[None], (n, *block.shape))
    mine = exchange(spread, PLANE).reshape(-1, block.shape[-1])
    return mine, swap(mine)


def scatter(own, other, n):
    got = swap(other)
    both = (own + got.astype(F32)).astype(BF)
    moved = exchange(both.reshape(n, -1, both.shape[-1]), PLANE)
    return jnp.sum(moved.astype(F32), axis=0)


def body(
    residual,
    ffn_gain,
    gate_weight,
    up_weight,
    down_weight,
    final_gain,
    head_weight,
    passage_ids,
    valid_counts,
):
    highest = lax.Precision.HIGHEST
    core = lax.axis_index("c")
    n = lax.axis_size(PLANE)
    n_dp = lax.axis_size("dp")
    n_mp = lax.axis_size(MP)
    own_rows = residual.astype(F32)
    normed_in = (own_rows * rms_scale(own_rows) * ffn_gain).astype(BF)
    member, valid = pool_masks(passage_ids[0], valid_counts[0])
    gate_up = jnp.concatenate([gate_weight, up_weight], axis=1)
    mine, theirs = gather(chip_rows(normed_in, core), n)
    residual8 = chip_rows(residual, core).astype(F32)
    gain8 = halves(final_gain[None, :], core, 1)[0]

    gu_own, gu_other = halves(gate_up, core, 0)
    gu = mm(mine, gu_own) + mm(theirs, gu_other)
    hid = gate_weight.shape[1]
    activated = (jax.nn.silu(gu[:, :hid]) * gu[:, hid:]).astype(BF)
    down_own, down_other = halves(down_weight, core, 1)
    other = mm(activated, down_other).astype(BF)
    hidden8 = residual8 + scatter(mm(activated, down_own), other, n)
    square = jnp.sum(hidden8 * hidden8, axis=1, keepdims=True)
    width = residual.shape[1]
    scale8 = lax.rsqrt((square + swap(square)) / width + 1e-05)
    normed8 = (hidden8 * scale8 * gain8).astype(BF)
    mine, theirs = gather(normed8, n)
    hidden = core_rows(hidden8, core)
    scale = rms_scale(hidden)

    head_own, head_other = halves(head_weight, core, 0)
    logits = mm(mine, head_own) + mm(theirs, head_other)
    positive = jnp.maximum(logits, 0.0)
    weights = jnp.log1p(positive)
    powered = valid[:, None] * weights**4
    pooled_sum = lax.dot_general(member, powered, (((0,), (0,)), ((), ())), precision=highest)
    term_weights = (1.0 + pooled_sum) ** 0.25 - 1.0
    local_mass = jnp.sum(term_weights, axis=0).reshape(-1, 128)
    first, second, third = (
        lax.ppermute(local_mass, "dp", [(i, (i + k) % n_dp) for i in range(n_dp)])
        for k in range(1, n_dp)
    )
    smooth = 1.0 + ((local_mass + second) + (first + third))
    log_smooth = jnp.log(smooth)
    sums = jnp.stack([jnp.sum(smooth, axis=0), jnp.sum(smooth * log_smooth, axis=0)])
    sums = exchange(jnp.broadcast_to(sums[None], (n_mp, 2, 128)), MP)
    slope = lax.optimization_barrier(valid[:, None] * weights**3 / (1.0 + positive))
    row_factor = jnp.dot(member, (1.0 + pooled_sum) ** (-0.75), precision=highest)
    slope = lax.optimization_barrier(slope * row_factor)
    sums = jnp.sum(jnp.sum(sums, axis=0), axis=1)
    total, spread = sums[0], sums[1]
    entropy = jnp.log(total) - spread / total
    slope_mass = jnp.log(total) - log_smooth.reshape(-1)
    slope_logit = lax.optimization_barrier((slope * slope_mass[None, :]).astype(BF))
    other = mm_t(slope_logit, head_other).astype(BF)
    own = lax.optimization_barrier(mm_t(slope_logit, head_own))
    slope_normed = core_rows(scatter(own, other, n), core)
    scaled_slope = slope_normed * final_gain
    grad_hidden = scale * scaled_slope - hidden * scale**3 * jnp.mean(
        scaled_slope * hidden, axis=-1, keepdims=True
    )
    return (term_weights, entropy, grad_hidden)


def solution(mesh):
    axes = Mesh(mesh.devices.reshape(mesh.shape["dp"], 8, 4, 2), ALL)
    placed = (
        P(ALL, None),
        P(),
        P(None, MP),
        P(None, MP),
        P(MP, None),
        P(),
        P(None, MP),
        P("dp", None),
        P("dp", None),
    )
    return jax.shard_map(
        body,
        mesh=axes,
        in_specs=placed,
        out_specs=(P("dp", MP), P(), P(ALL, None)),
        check_vma=False,
    )
```

```python
import jax
import jax.numpy as jnp
from jax import lax
from jax.sharding import Mesh, PartitionSpec as P


ALL = ("dp", "z", "y", "c")
MP = ("z", "y", "c")
BF = jnp.bfloat16
F32 = jnp.float32


def rms_scale(values):
    return lax.rsqrt(jnp.mean(values * values, axis=-1, keepdims=True) + 1e-05)


def pool_masks(ids, counts):
    slots = jnp.arange(counts.shape[0], dtype=jnp.int32)
    member = ids[:, None] == slots[None, :]
    starts = jnp.sum((ids[:, None] < slots[None, :]).astype(jnp.int32), axis=0)
    start_row = jnp.sum(jnp.where(member, starts[None, :], 0), axis=1)
    count_row = jnp.sum(jnp.where(member, counts[None, :], 0), axis=1)
    position = jnp.arange(ids.shape[0], dtype=jnp.int32) - start_row
    valid = (position < count_row).astype(F32)
    return (member.astype(F32), valid)


def swap(x):
    return lax.ppermute(x, "c", [(0, 1), (1, 0)])


def mm(a, b):
    return jnp.dot(a, b, preferred_element_type=F32)


def mm_t(a, b):
    return lax.dot_general(a, b, (((1,), (1,)), ((), ())), preferred_element_type=F32)


def halves(x, core, axis):
    size = x.shape[axis] // 2
    own = lax.dynamic_slice_in_dim(x, core * size, size, axis)
    other = lax.dynamic_slice_in_dim(x, (1 - core) * size, size, axis)
    return own, other


def chip_rows(x, core):
    own, other = halves(x, core, 1)
    got = swap(other)
    return jnp.where(core == 0, jnp.concatenate([own, got], 0), jnp.concatenate([got, own], 0))


def core_rows(x, core):
    own, other = halves(x, core, 0)
    got = swap(other)
    return jnp.where(core == 0, jnp.concatenate([own, got], 1), jnp.concatenate([got, own], 1))


def exchange(x, axes):
    return lax.all_to_all(x, axes, 0, 0)


def along_y(x, k):
    n = lax.axis_size("y")
    return lax.ppermute(x, "y", [(i, (i + k) % n) for i in range(n)])


def local_rows(x):
    nz, ny = lax.axis_size("z"), lax.axis_size("y")
    x = x.reshape(nz, ny, -1, *x.shape[1:])
    x = lax.dynamic_slice_in_dim(jnp.concatenate([x, x], axis=1), lax.axis_index("y"), ny, 1)
    return x.swapaxes(0, 1).reshape(-1, *x.shape[3:])


def gather(block):
    spread = jnp.broadcast_to(block[None], (lax.axis_size("z"), *block.shape))
    plane = exchange(spread, "z").reshape(-1, block.shape[-1])
    got = [along_y(plane, -k) for k in range(1, lax.axis_size("y"))]
    mine = jnp.concatenate([plane, *got], axis=0)
    return mine, swap(mine)


def both_halves(mine, theirs, weight, core):
    own, other = halves(weight, core, 0)
    first = lax.optimization_barrier(mm(mine, own))
    return first + mm(theirs, other)


def scatter(own, other):
    got = swap(other)
    ny, nz = lax.axis_size("y"), lax.axis_size("z")
    own, got = jnp.split(own, ny), jnp.split(got, ny)
    both = [a + b.astype(F32) for a, b in zip(own, got)]
    for k in range(1, ny):
        both[k] = along_y(both[k].astype(BF), k).astype(F32)
    plane = sum(both).astype(BF)
    moved = exchange(plane.reshape(nz, -1, plane.shape[-1]), "z")
    return jnp.sum(moved.astype(F32), axis=0)


def body(
    residual,
    ffn_gain,
    gate_weight,
    up_weight,
    down_weight,
    final_gain,
    head_weight,
    passage_ids,
    valid_counts,
):
    highest = lax.Precision.HIGHEST
    core = lax.axis_index("c")
    n_dp = lax.axis_size("dp")
    n_mp = lax.axis_size(MP)
    own_rows = residual.astype(F32)
    normed_in = (own_rows * rms_scale(own_rows) * ffn_gain).astype(BF)
    member, valid = pool_masks(passage_ids[0], valid_counts[0])
    member, valid = local_rows(member), local_rows(valid)
    gate_up = jnp.concatenate([gate_weight, up_weight], axis=1)
    mine, theirs = gather(chip_rows(normed_in, core))
    residual8 = chip_rows(residual, core).astype(F32)
    gain8 = halves(final_gain[None, :], core, 1)[0]

    gu = both_halves(mine, theirs, gate_up, core)
    hid = gate_weight.shape[1]
    activated = (jax.nn.silu(gu[:, :hid]) * gu[:, hid:]).astype(BF)
    down_own, down_other = halves(down_weight, core, 1)
    other = mm(activated, down_other).astype(BF)
    hidden8 = residual8 + scatter(mm(activated, down_own), other)
    square = jnp.sum(hidden8 * hidden8, axis=1, keepdims=True)
    width = residual.shape[1]
    scale8 = lax.rsqrt((square + swap(square)) / width + 1e-05)
    normed8 = (hidden8 * scale8 * gain8).astype(BF)
    mine, theirs = gather(normed8)
    hidden = core_rows(hidden8, core)
    scale = rms_scale(hidden)

    logits = both_halves(mine, theirs, head_weight, core)
    positive = jnp.maximum(logits, 0.0)
    weights = jnp.log1p(positive)
    powered = valid[:, None] * weights**4
    pooled_sum = lax.dot_general(member, powered, (((0,), (0,)), ((), ())), precision=highest)
    term_weights = (1.0 + pooled_sum) ** 0.25 - 1.0
    local_mass = jnp.sum(term_weights, axis=0).reshape(-1, 128)
    first, second, third = (
        lax.ppermute(local_mass, "dp", [(i, (i + k) % n_dp) for i in range(n_dp)])
        for k in range(1, n_dp)
    )
    smooth = 1.0 + ((local_mass + second) + (first + third))
    log_smooth = jnp.log(smooth)
    sums = jnp.stack([jnp.sum(smooth, axis=0), jnp.sum(smooth * log_smooth, axis=0)])
    sums = exchange(jnp.broadcast_to(sums[None], (n_mp, 2, 128)), MP)
    slope = lax.optimization_barrier(valid[:, None] * weights**3 / (1.0 + positive))
    row_factor = jnp.dot(member, (1.0 + pooled_sum) ** (-0.75), precision=highest)
    slope = lax.optimization_barrier(slope * row_factor)
    sums = jnp.sum(jnp.sum(sums, axis=0), axis=1)
    total, spread = sums[0], sums[1]
    entropy = jnp.log(total) - spread / total
    slope_mass = jnp.log(total) - log_smooth.reshape(-1)
    slope_logit = lax.optimization_barrier((slope * slope_mass[None, :]).astype(BF))
    head_own, head_other = halves(head_weight, core, 0)
    other = mm_t(slope_logit, head_other).astype(BF)
    own = lax.optimization_barrier(mm_t(slope_logit, head_own))
    slope_normed = core_rows(scatter(own, other), core)
    scaled_slope = slope_normed * final_gain
    grad_hidden = scale * scaled_slope - hidden * scale**3 * jnp.mean(
        scaled_slope * hidden, axis=-1, keepdims=True
    )
    return (term_weights, entropy, grad_hidden)


def solution(mesh):
    axes = Mesh(mesh.devices.reshape(mesh.shape["dp"], 8, 4, 2), ALL)
    placed = (
        P(ALL, None),
        P(),
        P(None, MP),
        P(None, MP),
        P(MP, None),
        P(),
        P(None, MP),
        P("dp", None),
        P("dp", None),
    )
    return jax.shard_map(
        body,
        mesh=axes,
        in_specs=placed,
        out_specs=(P("dp", MP), P(), P(ALL, None)),
        check_vma=False,
    )
```

```python
import jax
import jax.numpy as jnp
from jax import lax
from jax.sharding import Mesh, PartitionSpec as P


ALL = ("dp", "z", "y", "c")
MP = ("z", "y", "c")
BF = jnp.bfloat16
F32 = jnp.float32


def rms_scale(values):
    return lax.rsqrt(jnp.mean(values * values, axis=-1, keepdims=True) + 1e-05)


def pool_masks(ids, counts):
    slots = jnp.arange(counts.shape[0], dtype=jnp.int32)
    member = ids[:, None] == slots[None, :]
    starts = jnp.sum((ids[:, None] < slots[None, :]).astype(jnp.int32), axis=0)
    start_row = jnp.sum(jnp.where(member, starts[None, :], 0), axis=1)
    count_row = jnp.sum(jnp.where(member, counts[None, :], 0), axis=1)
    position = jnp.arange(ids.shape[0], dtype=jnp.int32) - start_row
    valid = (position < count_row).astype(F32)
    return (member.astype(F32), valid)


def swap(x):
    return lax.ppermute(x, "c", [(0, 1), (1, 0)])


def mm(a, b):
    return jnp.dot(a, b, preferred_element_type=F32)


def mm_t(a, b):
    return lax.dot_general(a, b, (((1,), (1,)), ((), ())), preferred_element_type=F32)


def halves(x, core, axis):
    size = x.shape[axis] // 2
    own = lax.dynamic_slice_in_dim(x, core * size, size, axis)
    other = lax.dynamic_slice_in_dim(x, (1 - core) * size, size, axis)
    return own, other


def chip_rows(x, core):
    own, other = halves(x, core, 1)
    got = swap(other)
    return jnp.where(core == 0, jnp.concatenate([own, got], 0), jnp.concatenate([got, own], 0))


def core_rows(x, core):
    own, other = halves(x, core, 0)
    got = swap(other)
    return jnp.where(core == 0, jnp.concatenate([own, got], 1), jnp.concatenate([got, own], 1))


def exchange(x, axes):
    return lax.all_to_all(x, axes, 0, 0)


def along_y(x, k):
    n = lax.axis_size("y")
    return lax.ppermute(x, "y", [(i, (i + k) % n) for i in range(n)])


def local_rows(x):
    nz, ny = lax.axis_size("z"), lax.axis_size("y")
    x = x.reshape(nz, ny, -1, *x.shape[1:])
    x = lax.dynamic_slice_in_dim(jnp.concatenate([x, x], axis=1), lax.axis_index("y"), ny, 1)
    return x.swapaxes(0, 1).reshape(-1, *x.shape[3:])


def gather(block):
    spread = jnp.broadcast_to(block[None], (lax.axis_size("z"), *block.shape))
    plane = exchange(spread, "z").reshape(-1, block.shape[-1])
    got = [along_y(plane, -k) for k in range(1, lax.axis_size("y"))]
    theirs = [swap(x) for x in (plane, *got)]
    return [lax.optimization_barrier(jnp.concatenate(x, axis=0)) for x in ([plane, *got], theirs)]


def both_halves(mine, theirs, own, other):
    first = lax.optimization_barrier(mm(mine, own))
    return first + mm(theirs, other)


def scatter(own, other):
    got = swap(other)
    ny, nz = lax.axis_size("y"), lax.axis_size("z")
    own, got = jnp.split(own, ny), jnp.split(got, ny)
    both = [a + b.astype(F32) for a, b in zip(own, got)]
    for k in range(1, ny):
        both[k] = along_y(both[k].astype(BF), k).astype(F32)
    plane = sum(both).astype(BF)
    moved = exchange(plane.reshape(nz, -1, plane.shape[-1]), "z")
    return jnp.sum(moved.astype(F32), axis=0)


def body(
    residual,
    ffn_gain,
    gate_weight,
    up_weight,
    down_weight,
    final_gain,
    head_weight,
    passage_ids,
    valid_counts,
):
    highest = lax.Precision.HIGHEST
    core = lax.axis_index("c")
    n_dp = lax.axis_size("dp")
    n_mp = lax.axis_size(MP)
    own_rows = residual.astype(F32)
    normed_in = (own_rows * rms_scale(own_rows) * ffn_gain).astype(BF)
    member, valid = pool_masks(passage_ids[0], valid_counts[0])
    member, valid = local_rows(member), local_rows(valid)
    gate_up = jnp.concatenate([gate_weight, up_weight], axis=1)
    mine, theirs = gather(chip_rows(normed_in, core))
    residual8 = chip_rows(residual, core).astype(F32)
    gain8 = halves(final_gain[None, :], core, 1)[0]

    gu = both_halves(mine, theirs, *halves(gate_up, core, 0))
    hid = gate_weight.shape[1]
    activated = (jax.nn.silu(gu[:, :hid]) * gu[:, hid:]).astype(BF)
    down_own, down_other = halves(down_weight, core, 1)
    other = mm(activated, down_other).astype(BF)
    hidden8 = residual8 + scatter(mm(activated, down_own), other)
    square = jnp.sum(hidden8 * hidden8, axis=1, keepdims=True)
    width = residual.shape[1]
    scale8 = lax.rsqrt((square + swap(square)) / width + 1e-05)
    normed8 = (hidden8 * scale8 * gain8).astype(BF)
    mine, theirs = gather(normed8)
    hidden = core_rows(hidden8, core)
    scale = rms_scale(hidden)

    head_own, head_other = lax.optimization_barrier(halves(head_weight, core, 0))
    logits = both_halves(mine, theirs, head_own, head_other)
    positive = jnp.maximum(logits, 0.0)
    weights = jnp.log1p(positive)
    powered = valid[:, None] * weights**4
    pooled_sum = lax.dot_general(member, powered, (((0,), (0,)), ((), ())), precision=highest)
    term_weights = (1.0 + pooled_sum) ** 0.25 - 1.0
    local_mass = jnp.sum(term_weights, axis=0).reshape(-1, 128)
    first, second, third = (
        lax.ppermute(local_mass, "dp", [(i, (i + k) % n_dp) for i in range(n_dp)])
        for k in range(1, n_dp)
    )
    smooth = 1.0 + ((local_mass + second) + (first + third))
    log_smooth = jnp.log(smooth)
    sums = jnp.stack([jnp.sum(smooth, axis=0), jnp.sum(smooth * log_smooth, axis=0)])
    sums = exchange(jnp.broadcast_to(sums[None], (n_mp, 2, 128)), MP)
    slope = lax.optimization_barrier(valid[:, None] * weights**3 / (1.0 + positive))
    row_factor = jnp.dot(member, (1.0 + pooled_sum) ** (-0.75), precision=highest)
    slope = lax.optimization_barrier(slope * row_factor)
    sums = jnp.sum(jnp.sum(sums, axis=0), axis=1)
    total, spread = sums[0], sums[1]
    entropy = jnp.log(total) - spread / total
    slope_mass = jnp.log(total) - log_smooth.reshape(-1)
    slope_logit = lax.optimization_barrier((slope * slope_mass[None, :]).astype(BF))
    other = mm_t(slope_logit, head_other).astype(BF)
    own = lax.optimization_barrier(mm_t(slope_logit, head_own))
    slope_normed = core_rows(scatter(own, other), core)
    scaled_slope = slope_normed * final_gain
    grad_hidden = scale * scaled_slope - hidden * scale**3 * jnp.mean(
        scaled_slope * hidden, axis=-1, keepdims=True
    )
    return (term_weights, entropy, grad_hidden)


def solution(mesh):
    axes = Mesh(mesh.devices.reshape(mesh.shape["dp"], 8, 4, 2), ALL)
    placed = (
        P(ALL, None),
        P(),
        P(None, MP),
        P(None, MP),
        P(MP, None),
        P(),
        P(None, MP),
        P("dp", None),
        P("dp", None),
    )
    return jax.shard_map(
        body,
        mesh=axes,
        in_specs=placed,
        out_specs=(P("dp", MP), P(), P(ALL, None)),
        check_vma=False,
    )
```

```python
import jax
import jax.numpy as jnp
from jax import lax
from jax.sharding import Mesh, PartitionSpec as P


ALL = ("dp", "z", "y", "c")
MP = ("z", "y", "c")
BF = jnp.bfloat16
F32 = jnp.float32


def rms_scale(values):
    return lax.rsqrt(jnp.mean(values * values, axis=-1, keepdims=True) + 1e-05)


def pool_masks(ids, counts):
    slots = jnp.arange(counts.shape[0], dtype=jnp.int32)
    member = ids[:, None] == slots[None, :]
    starts = jnp.sum((ids[:, None] < slots[None, :]).astype(jnp.int32), axis=0)
    start_row = jnp.sum(jnp.where(member, starts[None, :], 0), axis=1)
    count_row = jnp.sum(jnp.where(member, counts[None, :], 0), axis=1)
    position = jnp.arange(ids.shape[0], dtype=jnp.int32) - start_row
    valid = (position < count_row).astype(F32)
    return (member.astype(F32), valid)


def swap(x):
    return lax.ppermute(x, "c", [(0, 1), (1, 0)])


def mm(a, b):
    return jnp.dot(a, b, preferred_element_type=F32)


def mm_t(a, b):
    return lax.dot_general(a, b, (((1,), (1,)), ((), ())), preferred_element_type=F32)


def halves(x, core, axis):
    size = x.shape[axis] // 2
    own = lax.dynamic_slice_in_dim(x, core * size, size, axis)
    other = lax.dynamic_slice_in_dim(x, (1 - core) * size, size, axis)
    return own, other


def chip_rows(x, core):
    own, other = halves(x, core, 1)
    got = swap(other)
    return jnp.where(core == 0, jnp.concatenate([own, got], 0), jnp.concatenate([got, own], 0))


def core_rows(x, core):
    own, other = halves(x, core, 0)
    got = swap(other)
    return jnp.where(core == 0, jnp.concatenate([own, got], 1), jnp.concatenate([got, own], 1))


def exchange(x, axes):
    return lax.all_to_all(x, axes, 0, 0)


def along_y(x, k):
    n = lax.axis_size("y")
    return lax.ppermute(x, "y", [(i, (i + k) % n) for i in range(n)])


def local_rows(x):
    nz, ny = lax.axis_size("z"), lax.axis_size("y")
    x = x.reshape(nz, ny, -1, *x.shape[1:])
    x = lax.dynamic_slice_in_dim(jnp.concatenate([x, x], axis=1), lax.axis_index("y"), ny, 1)
    return x.swapaxes(0, 1).reshape(-1, *x.shape[3:])


def gather(block):
    spread = jnp.broadcast_to(block[None], (lax.axis_size("z"), *block.shape))
    plane = exchange(spread, "z").reshape(-1, block.shape[-1])
    got = [along_y(plane, -k) for k in range(1, lax.axis_size("y"))]
    theirs = [swap(x) for x in (plane, *got)]
    return [lax.optimization_barrier(jnp.concatenate(x, axis=0)) for x in ([plane, *got], theirs)]


def both_halves(mine, theirs, own, other):
    first = lax.optimization_barrier(mm(mine, own))
    return first + mm(theirs, other)


def scatter(own, other):
    got = swap(other)
    ny, nz = lax.axis_size("y"), lax.axis_size("z")
    own, got = jnp.split(own, ny), jnp.split(got, ny)
    both = [a + b.astype(F32) for a, b in zip(own, got)]
    for k in range(1, ny):
        both[k] = along_y(both[k].astype(BF), k).astype(F32)
    plane = sum(both).astype(BF)
    moved = exchange(plane.reshape(nz, -1, plane.shape[-1]), "z")
    return jnp.sum(moved.astype(F32), axis=0)


def body(
    residual,
    ffn_gain,
    gate_weight,
    up_weight,
    down_weight,
    final_gain,
    head_weight,
    passage_ids,
    valid_counts,
):
    highest = lax.Precision.HIGHEST
    core = lax.axis_index("c")
    n_dp = lax.axis_size("dp")
    n_mp = lax.axis_size(MP)
    got = swap(residual)
    half = residual.shape[1] // 2

    def chip_order(a, b):
        return jnp.where(core == 0, jnp.concatenate([a, b], 0), jnp.concatenate([b, a], 0))

    def columns(x):
        return jnp.where(core == 0, x[..., :half], x[..., half:])

    scale_in = chip_order(rms_scale(residual.astype(F32)), rms_scale(got.astype(F32)))
    block = chip_order(columns(residual), columns(got))
    normed_in = (block.astype(F32) * scale_in * columns(ffn_gain)).astype(BF)
    member, valid = pool_masks(passage_ids[0], valid_counts[0])
    member, valid = local_rows(member), local_rows(valid)
    gate_up = jnp.concatenate([gate_weight, up_weight], axis=1)
    mine, theirs = gather(normed_in)
    residual8 = chip_rows(residual, core).astype(F32)
    gain8 = halves(final_gain[None, :], core, 1)[0]

    gu = both_halves(mine, theirs, *halves(gate_up, core, 0))
    hid = gate_weight.shape[1]
    activated = (jax.nn.silu(gu[:, :hid]) * gu[:, hid:]).astype(BF)
    down_own, down_other = halves(down_weight, core, 1)
    other = mm(activated, down_other).astype(BF)
    hidden8 = residual8 + scatter(mm(activated, down_own), other)
    square = jnp.sum(hidden8 * hidden8, axis=1, keepdims=True)
    width = residual.shape[1]
    scale8 = lax.rsqrt((square + swap(square)) / width + 1e-05)
    normed8 = (hidden8 * scale8 * gain8).astype(BF)
    mine, theirs = gather(normed8)
    hidden = core_rows(hidden8, core)
    scale = rms_scale(hidden)

    head_own, head_other = lax.optimization_barrier(halves(head_weight, core, 0))
    logits = lax.optimization_barrier(both_halves(mine, theirs, head_own, head_other))
    positive = jnp.maximum(logits, 0.0)
    weights = jnp.log1p(positive)
    powered = valid[:, None] * weights**4
    pooled_sum = lax.dot_general(member, powered, (((0,), (0,)), ((), ())), precision=highest)
    term_weights = (1.0 + pooled_sum) ** 0.25 - 1.0
    local_mass = jnp.sum(term_weights, axis=0).reshape(-1, 128)
    first, second, third = (
        lax.ppermute(local_mass, "dp", [(i, (i + k) % n_dp) for i in range(n_dp)])
        for k in range(1, n_dp)
    )
    smooth = 1.0 + ((local_mass + second) + (first + third))
    log_smooth = jnp.log(smooth)
    sums = jnp.stack([jnp.sum(smooth, axis=0), jnp.sum(smooth * log_smooth, axis=0)])
    sums = exchange(jnp.broadcast_to(sums[None], (n_mp, 2, 128)), MP)
    row_factor = jnp.dot(member, (1.0 + pooled_sum) ** (-0.75), precision=highest)
    slope = lax.optimization_barrier(valid[:, None] * weights**3 * row_factor / (1.0 + positive))
    sums = jnp.sum(jnp.sum(sums, axis=0), axis=1)
    total, spread = sums[0], sums[1]
    entropy = jnp.log(total) - spread / total
    slope_mass = jnp.log(total) - log_smooth.reshape(-1)
    slope_logit = lax.optimization_barrier((slope * slope_mass[None, :]).astype(BF))
    other = mm_t(slope_logit, head_other).astype(BF)
    own = lax.optimization_barrier(mm_t(slope_logit, head_own))
    slope_normed = core_rows(scatter(own, other), core)
    scaled_slope = slope_normed * final_gain
    grad_hidden = scale * scaled_slope - hidden * scale**3 * jnp.mean(
        scaled_slope * hidden, axis=-1, keepdims=True
    )
    return (term_weights, entropy, grad_hidden)


def solution(mesh):
    axes = Mesh(mesh.devices.reshape(mesh.shape["dp"], 8, 4, 2), ALL)
    placed = (
        P(ALL, None),
        P(),
        P(None, MP),
        P(None, MP),
        P(MP, None),
        P(),
        P(None, MP),
        P("dp", None),
        P("dp", None),
    )
    return jax.shard_map(
        body,
        mesh=axes,
        in_specs=placed,
        out_specs=(P("dp", MP), P(), P(ALL, None)),
        check_vma=False,
    )
```

```python
import jax
import jax.numpy as jnp
from jax import lax
from jax.sharding import Mesh, PartitionSpec as P


ALL = ("dp", "z", "y", "c")
MP = ("z", "y", "c")
BF = jnp.bfloat16
F32 = jnp.float32


def rms_scale(values):
    return lax.rsqrt(jnp.mean(values * values, axis=-1, keepdims=True) + 1e-05)


def pool_masks(ids, counts):
    slots = jnp.arange(counts.shape[0], dtype=jnp.int32)
    member = ids[:, None] == slots[None, :]
    starts = jnp.sum((ids[:, None] < slots[None, :]).astype(jnp.int32), axis=0)
    start_row = jnp.sum(jnp.where(member, starts[None, :], 0), axis=1)
    count_row = jnp.sum(jnp.where(member, counts[None, :], 0), axis=1)
    position = jnp.arange(ids.shape[0], dtype=jnp.int32) - start_row
    valid = (position < count_row).astype(F32)
    return (member.astype(F32), valid)


def swap(x):
    return lax.ppermute(x, "c", [(0, 1), (1, 0)])


def mm(a, b):
    return jnp.dot(a, b, preferred_element_type=F32)


def mm_t(a, b):
    return lax.dot_general(a, b, (((1,), (1,)), ((), ())), preferred_element_type=F32)


def halves(x, core, axis):
    size = x.shape[axis] // 2
    own = lax.dynamic_slice_in_dim(x, core * size, size, axis)
    other = lax.dynamic_slice_in_dim(x, (1 - core) * size, size, axis)
    return own, other


def chip_rows(x, core):
    own, other = halves(x, core, 1)
    got = swap(other)
    return jnp.where(core == 0, jnp.concatenate([own, got], 0), jnp.concatenate([got, own], 0))


def core_rows(x, core):
    own, other = halves(x, core, 0)
    got = swap(other)
    return jnp.where(core == 0, jnp.concatenate([own, got], 1), jnp.concatenate([got, own], 1))


def exchange(x, axes):
    return lax.all_to_all(x, axes, 0, 0)


def along_y(x, k):
    n = lax.axis_size("y")
    return lax.ppermute(x, "y", [(i, (i + k) % n) for i in range(n)])


def local_rows(x):
    nz, ny = lax.axis_size("z"), lax.axis_size("y")
    x = x.reshape(nz, ny, -1, *x.shape[1:])
    x = lax.dynamic_slice_in_dim(jnp.concatenate([x, x], axis=1), lax.axis_index("y"), ny, 1)
    return x.swapaxes(0, 1).reshape(-1, *x.shape[3:])


def gather(block):
    spread = jnp.broadcast_to(block[None], (lax.axis_size("z"), *block.shape))
    plane = exchange(spread, "z").reshape(-1, block.shape[-1])
    got = [along_y(plane, -k) for k in range(1, lax.axis_size("y"))]
    theirs = [swap(x) for x in (plane, *got)]
    return [lax.optimization_barrier(jnp.concatenate(x, axis=0)) for x in ([plane, *got], theirs)]


def both_halves(mine, theirs, own, other):
    first = lax.optimization_barrier(mm(mine, own))
    return first + mm(theirs, other)


def scatter(own, other):
    got = swap(other)
    ny, nz = lax.axis_size("y"), lax.axis_size("z")
    own, got = jnp.split(own, ny), jnp.split(got, ny)
    both = [a + b.astype(F32) for a, b in zip(own, got)]
    for k in range(1, ny):
        both[k] = along_y(both[k].astype(BF), k).astype(F32)
    plane = sum(both).astype(BF)
    moved = exchange(plane.reshape(nz, -1, plane.shape[-1]), "z")
    return jnp.sum(moved.astype(F32), axis=0)


def body(
    residual,
    ffn_gain,
    gate_weight,
    up_weight,
    down_weight,
    final_gain,
    head_weight,
    passage_ids,
    valid_counts,
):
    highest = lax.Precision.HIGHEST
    core = lax.axis_index("c")
    n_dp = lax.axis_size("dp")
    n_mp = lax.axis_size(MP)
    got = swap(residual)
    half = residual.shape[1] // 2

    def chip_order(a, b):
        return jnp.where(core == 0, jnp.concatenate([a, b], 0), jnp.concatenate([b, a], 0))

    def columns(x):
        return jnp.where(core == 0, x[..., :half], x[..., half:])

    scale_in = rms_scale(chip_order(residual, got).astype(F32))
    block = chip_order(columns(residual), columns(got)).astype(F32)
    normed_in = (block * scale_in * halves(ffn_gain[None, :], core, 1)[0]).astype(BF)
    member, valid = pool_masks(passage_ids[0], valid_counts[0])
    member, valid = local_rows(member), local_rows(valid)
    gate_up = jnp.concatenate([gate_weight, up_weight], axis=1)
    mine, theirs = gather(normed_in)
    residual8 = chip_rows(residual, core).astype(F32)
    gain8 = halves(final_gain[None, :], core, 1)[0]

    gu = both_halves(mine, theirs, *halves(gate_up, core, 0))
    hid = gate_weight.shape[1]
    activated = (jax.nn.silu(gu[:, :hid]) * gu[:, hid:]).astype(BF)
    down_own, down_other = halves(down_weight, core, 1)
    other = mm(activated, down_other).astype(BF)
    hidden8 = residual8 + scatter(mm(activated, down_own), other)
    square = jnp.sum(hidden8 * hidden8, axis=1, keepdims=True)
    width = residual.shape[1]
    scale8 = lax.rsqrt((square + swap(square)) / width + 1e-05)
    normed8 = (hidden8 * scale8 * gain8).astype(BF)
    mine, theirs = gather(normed8)
    hidden = core_rows(hidden8, core)
    scale = rms_scale(hidden)

    head_own, head_other = lax.optimization_barrier(halves(head_weight, core, 0))
    logits = lax.optimization_barrier(both_halves(mine, theirs, head_own, head_other))
    positive = jnp.maximum(logits, 0.0)
    weights = jnp.log1p(positive)
    powered = valid[:, None] * weights**4
    pooled_sum = lax.dot_general(member, powered, (((0,), (0,)), ((), ())), precision=highest)
    term_weights = (1.0 + pooled_sum) ** 0.25 - 1.0
    local_mass = jnp.sum(term_weights, axis=0).reshape(-1, 128)
    first, second, third = (
        lax.ppermute(local_mass, "dp", [(i, (i + k) % n_dp) for i in range(n_dp)])
        for k in range(1, n_dp)
    )
    smooth = 1.0 + ((local_mass + second) + (first + third))
    log_smooth = jnp.log(smooth)
    sums = jnp.stack([jnp.sum(smooth, axis=0), jnp.sum(smooth * log_smooth, axis=0)])
    sums = exchange(jnp.broadcast_to(sums[None], (n_mp, 2, 128)), MP)
    row_factor = jnp.dot(member, (1.0 + pooled_sum) ** (-0.75), precision=highest)
    slope = lax.optimization_barrier(valid[:, None] * weights**3 * row_factor / (1.0 + positive))
    sums = jnp.sum(jnp.sum(sums, axis=0), axis=1)
    total, spread = sums[0], sums[1]
    entropy = jnp.log(total) - spread / total
    slope_mass = jnp.log(total) - log_smooth.reshape(-1)
    slope_logit = lax.optimization_barrier((slope * slope_mass[None, :]).astype(BF))
    other = mm_t(slope_logit, head_other).astype(BF)
    own = lax.optimization_barrier(mm_t(slope_logit, head_own))
    slope_normed = core_rows(scatter(own, other), core)
    scaled_slope = slope_normed * final_gain
    grad_hidden = scale * scaled_slope - hidden * scale**3 * jnp.mean(
        scaled_slope * hidden, axis=-1, keepdims=True
    )
    return (term_weights, entropy, grad_hidden)


def solution(mesh):
    axes = Mesh(mesh.devices.reshape(mesh.shape["dp"], 8, 4, 2), ALL)
    placed = (
        P(ALL, None),
        P(),
        P(None, MP),
        P(None, MP),
        P(MP, None),
        P(),
        P(None, MP),
        P("dp", None),
        P("dp", None),
    )
    return jax.shard_map(
        body,
        mesh=axes,
        in_specs=placed,
        out_specs=(P("dp", MP), P(), P(ALL, None)),
        check_vma=False,
    )
```
